256 devices in a mesh: client: 32 (over z_lo, y, core), mp: 8 (over x, z_hi).
Axes of the slice: x: 4, y: 4, z: 8 (z_hi: 2, z_lo: 4; z = z_hi * 4 + z_lo), core: 2. Of those that a mesh axis runs over, the one named last changes fastest.
Arguments:
- hidden: bfloat16 [32, 4, 128, 7168], P('client', None, None, 'mp'), may hold values from -6 to 6
- weight: bfloat16 [32, 7168, 2048], P('client', 'mp'), may hold values from -0.0625 to 0.0625
- target: bfloat16 [32, 4, 128, 2048], P('client', None, 'mp'), may hold values from -6 to 6
- router_prob: float32 [32, 4, 128], P('client', None, 'mp'), may hold values from 0.2 to 1
- routes: int32 [32, 4, 128, 2], P('client', None, 'mp'), may hold values from 0 to 7, all different within a row
- assign: int32 [32, 1], replicated, may hold values from 0 to 3
Outputs:
- merged_weight: bfloat16 [32, 7168, 2048], P('client', 'mp')
The draws below stay inside these ranges and needn't reach their ends.
Inputs may be any that keep to these rules, and one draw needn't show every extreme that they name: `routes`: each token names two different experts; the given weights are those of expert 0. `assign`: every cluster has at least one client.
All inputs are finite; a program needn't handle non-finite values.
Results may differ from the reference program's by a relative error of at most 0.0044.
The reference program's roundings to bfloat16 on the way (of `grad_out`, `a_weight` and `merged`) count: a program that leaves them out, or rounds other values in their place, can miss the bound.
Values may be sent and summed in bfloat16 or wider, within the bound.
A program may use at most 128 MiB of HBM per device.

```python
import jax
import jax.numpy as jnp
from jax import lax

D = 2048
FFW = 7168
EXPERTS = 8
NB = 4
TOKB = 128
CLUSTERS = 4
CLIENTS = 32


def shard_levels(stream_key, shape, pieces, low, largest):
    def one(dim, parts):
        draws = jax.random.uniform(jax.random.fold_in(jax.random.fold_in(stream_key, 6), dim), (parts,), jnp.float32, low / len(pieces), largest / len(pieces))
        return jnp.repeat(jnp.exp(draws), shape[dim] // parts).reshape((-1,) + (1,) * (len(shape) - dim - 1))

    gain = one(*pieces[0])
    for cut in pieces[1:]:
        gain = gain * one(*cut)
    return gain


def picks_of(rng, rows, amount, top, lift):
    ranking = jax.random.permutation(jax.random.fold_in(rng, 1), amount)
    boost = ranking
    for power in range(3):
        boost = boost * boost // amount
    boost = boost * lift // amount
    tickets = jax.random.randint(jax.random.fold_in(rng, 2), (rows, amount), 0, 4096) + boost
    fixed_rows = jax.random.permutation(jax.random.fold_in(rng, 3), rows)[jnp.arange(amount) % rows]
    tickets = jnp.where(jnp.arange(rows)[:, None] == fixed_rows[None, :], 1 << 14, tickets)
    merit = tickets * amount + jnp.arange(amount)
    return lax.top_k(merit.astype(jnp.int32), top)[1].astype(jnp.int32)


def bell_draw(rng, extent, scale, bound, split=(), held_as=jnp.bfloat16):
    array = scale * jax.random.normal(rng, extent, jnp.float32)
    if split:
        array = array * shard_levels(rng, extent, split, -0.22, 0.18)
    return jnp.clip(array, -bound, bound).astype(held_as)


def setup_inputs(seed: int = 0) -> dict:
    key_list = jax.random.split(jax.random.key(seed), 7)
    return {
        "hidden": bell_draw(key_list[0], (CLIENTS, NB, TOKB, FFW), 1.0, 6.0, ((0, 32), (3, 8))),
        "weight": bell_draw(key_list[1], (CLIENTS, FFW, D), FFW ** -0.5, 0.0625, ((0, 32), (1, 8))),
        "target": bell_draw(key_list[2], (CLIENTS, NB, TOKB, D), 1.0, 6.0, ((0, 32), (2, 8))),
        "router_prob": jnp.clip(0.2 + 0.8 * jax.random.uniform(key_list[3], (CLIENTS, NB, TOKB), jnp.float32) ** shard_levels(key_list[3], (CLIENTS, NB, TOKB), ((0, 32), (2, 8)), -0.2, 0.2), 0.2, 1.0),
        "routes": picks_of(key_list[4], CLIENTS * NB * TOKB, EXPERTS, 2, 4096).reshape((CLIENTS, NB, TOKB, 2)),
        "assign": picks_of(key_list[5], CLIENTS, CLUSTERS, 1, 2048),
    }


EPS = 1e-6
FLOOR = 0.1


def client_fisher(hid, wgt, tgt, prob, rts):
    fisher = jnp.zeros((FFW, D), jnp.float32)
    for batch in range(NB):
        outputs = jnp.dot(hid[batch], wgt, preferred_element_type=jnp.float32)
        token_weight = jnp.where(jnp.any(rts[batch] == 0, axis=-1), prob[batch], 0.0).astype(jnp.float32)
        grad_out = (token_weight[:, None] * (outputs - tgt[batch].astype(jnp.float32))).astype(jnp.bfloat16)
        grad = jnp.dot(hid[batch].T, grad_out, preferred_element_type=jnp.float32)
        fisher = fisher + grad * grad
    return fisher


def reference(hidden, weight, target, router_prob, routes, assign):
    def accumulate(carry, items):
        num_acc, den_acc = carry
        hid, wgt, tgt, prob, rts, cluster = items
        fisher = client_fisher(hid, wgt, tgt, prob, rts)
        mean_fisher = jnp.sum(fisher) / (FFW * D)
        a_weight = (fisher / (mean_fisher + EPS) + FLOOR).astype(jnp.bfloat16)
        a_float = a_weight.astype(jnp.float32)
        num_acc = num_acc.at[cluster[0]].add(a_float * wgt.astype(jnp.float32))
        den_acc = den_acc.at[cluster[0]].add(a_float)
        return (num_acc, den_acc), None

    start = (jnp.zeros((CLUSTERS, FFW, D), jnp.float32), jnp.zeros((CLUSTERS, FFW, D), jnp.float32))
    (num_acc, den_acc), _ = lax.scan(accumulate, start, (hidden, weight, target, router_prob, routes, assign))
    merged = (num_acc / den_acc).astype(jnp.bfloat16)
    return merged[assign[:, 0]]
```

```python
import functools

import jax
import jax.numpy as jnp
from jax import lax
from jax.experimental import pallas as pl
from jax.experimental.pallas import tpu as pltpu
from jax.sharding import PartitionSpec as P

D = 2048
FFW = 7168
NB = 4
CLUSTERS = 4
EPS = 1e-06
FLOOR = 0.1

F = 896
TOK = 128
OWN = 112
G16 = 16
NG = OWN // G16
NS = 2 * NG
HALF = D // 2
QUART = D // 4
WMAX = 0.0625
CODE = 32760.0 / WMAX

MESH = pl.DeviceIdType.MESH
f32 = jnp.float32
bf16 = jnp.bfloat16


def rcopy(src, dst, send, recv, device):
    return pltpu.make_async_remote_copy(
        src_ref=src, dst_ref=dst, send_sem=send, recv_sem=recv, device_id=device, device_id_type=MESH
    )


def kernel(
    hid, w, tgt, tw, mask, cluster, out,
    hid_t, y_f32, own, y_send, y_recv, z_send, z_recv, grad_out, fisher, sums, a_send, a_recv, w_recv,
    num, den, m_send, d_send, m_recv, d_recv, merged, picked,
    w_s, w_r, y_s, y_r, z_s, z_r, zg_s, zg_r, xg_s, xg_r, t_s, t_r, a_s, a_r, c_s, c_r, b_s, b_r, o_s, o_r, l_s,
):
    c = lax.axis_index("client")
    m = lax.axis_index("mp")
    zl, q = c // 8, c % 8
    xx, zh = m // 2, m % 2

    def plane(k):
        return (zl * 8 + k, m)

    def group(k):
        return (c, k)

    def line(k):
        return (k * 8 + q, m)

    barrier = pltpu.get_barrier_semaphore()
    for k in range(1, 8):
        pl.semaphore_signal(barrier, inc=1, device_id=plane((q + k) % 8), device_id_type=MESH)
        pl.semaphore_signal(barrier, inc=1, device_id=group((m + k) % 8), device_id_type=MESH)

    for k in (1, 3):
        pl.semaphore_signal(barrier, inc=1, device_id=line((zl + k) % 4), device_id_type=MESH)
    pl.semaphore_wait(barrier, 16)

    def w_copy(k, slot):
        rows = pl.ds(pl.multiple_of(k * OWN, 16), OWN)
        return rcopy(w.at[rows], w_recv.at[slot], w_s.at[k], w_r.at[slot], plane(k))

    def y_copy(b, k, slot):
        rows = pl.ds(pl.multiple_of(k * 32, 32), 32)
        return rcopy(
            y_send.at[b, rows], y_recv.at[b, slot], y_s.at[b, k], y_r.at[b, slot], group(k * 2 + zh)
        )

    def y_batch(b, _):
        for n in range(4):
            cols = pl.ds(n * QUART, QUART)
            y_f32[:, cols] = jnp.dot(hid[b], w[:, cols], preferred_element_type=f32)
            y_send[b, :, cols] = y_f32[:, cols].astype(bf16)
        own[b] = y_f32[pl.ds(pl.multiple_of(xx * 32, 32), 32), :]
        for k in range(1, 4):
            y_copy(b, (xx + k) % 4, xx).start()
        return 0

    lax.fori_loop(0, NB, y_batch, 0)

    for k in range(1, 8):
        w_copy((q + k) % 8, q).start()

    def prepare(b, _):
        hid_t[b] = hid[b].T
        return 0

    lax.fori_loop(0, NB, prepare, 0)

    def clear(r, _):
        rows = pl.ds(pl.multiple_of(r * 16, 16), 16)
        fisher[rows] = jnp.zeros((16, D), f32)
        return 0

    lax.fori_loop(0, F // 16, clear, 0)
    sums[m] = jnp.zeros((8, 256), f32)

    def keep_w(r, _):
        w_recv[q, pl.ds(pl.multiple_of(r * 16, 16), 16)] = w[pl.ds(pl.multiple_of(q * OWN + r * 16, 16), 16)]
        return 0

    lax.fori_loop(0, NG, keep_w, 0)

    mine = pl.ds(pl.multiple_of(m * 16, 16), 16)
    theirs = pl.ds(pl.multiple_of((xx * 2 + 1 - zh) * 16, 16), 16)
    partner = group(xx * 2 + 1 - zh)

    def z_copy(b):
        return rcopy(z_send.at[b], z_recv.at[b], z_s.at[b], z_r.at[b], partner)

    def zg_copy(b, rows):
        return rcopy(grad_out.at[b, rows], grad_out.at[b, rows], zg_s.at[b], zg_r.at[b], partner)

    def xg_copy(b, k, block):
        rows = pl.ds(pl.multiple_of(block * 32, 32), 32)
        return rcopy(
            grad_out.at[b, rows], grad_out.at[b, rows], xg_s.at[b, k], xg_r.at[b, block], group(k * 2 + zh)
        )

    def step_x(b):
        total = own[b]
        for k in range(1, 4):
            slot = (xx + k) % 4
            y_copy(b, slot, slot).wait_recv()
            total = total + y_recv[b, slot].astype(f32)
        own[b] = total
        z_send[b] = own[b, pl.ds(pl.multiple_of((1 - zh) * 16, 16), 16)].astype(bf16)
        z_copy(b).start()

    def step_z(b):
        z_copy(b).wait_recv()
        y = own[b, pl.ds(pl.multiple_of(zh * 16, 16), 16)] + z_recv[b].astype(f32)
        grad_out[b, mine] = (tw[b][:, :1] * (y - tgt[b].astype(f32))).astype(bf16)
        zg_copy(b, mine).start()

    def step_g(b):
        zg_copy(b, theirs).wait_recv()
        for k in range(1, 4):
            xg_copy(b, (xx + k) % 4, xx).start()

    def step_f(b):
        for k in range(1, 4):
            slot = (xx + k) % 4
            xg_copy(b, slot, slot).wait_recv()

        def tile(n, _):
            cols = pl.ds(pl.multiple_of(n * 256, 256), 256)
            g = jnp.dot(hid_t[b], grad_out[b, :, cols], preferred_element_type=f32)
            g = g * g
            fisher[:, cols] += g
            sums[m] += g.reshape(F // 8, 8, 256).sum(0)
            return 0

        lax.fori_loop(0, D // 256, tile, 0)

    def mp_step(t, _):
        pl.when(t < NB)(lambda: step_x(t))
        pl.when((t >= 1) & (t < NB + 1))(lambda: step_z(t - 1))
        pl.when((t >= 2) & (t < NB + 2))(lambda: step_g(t - 2))
        pl.when(t >= 3)(lambda: step_f(t - 3))
        return 0

    lax.fori_loop(0, NB + 3, mp_step, 0)

    def t_copy(k, slot):
        return rcopy(sums.at[slot], sums.at[slot], t_s.at[k], t_r.at[slot], group(k))

    for k in range(1, 8):
        t_copy((m + k) % 8, m).start()
    for k in range(1, 8):
        slot = (m + k) % 8
        t_copy(slot, slot).wait_recv()
    total = sums[0]
    for k in range(1, 8):
        total = total + sums[k]
    mean = jnp.sum(total) / (FFW * D)
    scale = 1.0 / jnp.full((8, 128), mean + EPS, f32)
    scale = scale[:1, :1]

    def a_copy(r, k, slot):
        src = pl.ds(pl.multiple_of(k * OWN + r * 16, 16), 16)
        dst = pl.ds(pl.multiple_of(r * 16, 16), 16)
        return rcopy(a_send.at[src], a_recv.at[slot, dst], a_s.at[k, r], a_r.at[slot, r], plane(k))

    def a_group(r, _):
        for k in range(1, 8):
            peer = (q + k) % 8
            rows = pl.ds(pl.multiple_of(peer * OWN + r * 16, 16), 16)
            a_send[rows] = (fisher[rows] * scale + FLOOR).astype(bf16)
            a_copy(r, peer, q).start()
        rows = pl.ds(pl.multiple_of(q * OWN + r * 16, 16), 16)
        a_recv[q, pl.ds(pl.multiple_of(r * 16, 16), 16)] = (fisher[rows] * scale + FLOOR).astype(bf16)
        return 0

    lax.fori_loop(0, NG, a_group, 0)

    for k in range(1, 8):
        slot = (q + k) % 8
        w_copy(slot, slot).wait_recv()

    def where(j):
        r, h = j // 2, j % 2
        return pl.ds(pl.multiple_of(r * 16, 16), 16), r, h

    def own_sums(j):
        rows, r, h = where(j)

        @pl.when(h == 0)
        def _():
            for k in range(1, 8):
                slot = (q + k) % 8
                a_copy(r, slot, slot).wait_recv()

        def tile(n, _):
            cols = pl.ds(pl.multiple_of(h * HALF + n * 256, 256), 256)
            nums = [jnp.zeros((16, 256), f32)] * CLUSTERS
            dens = [jnp.zeros((16, 256), f32)] * CLUSTERS
            for s in range(8):
                a = a_recv[s, rows, cols].astype(f32)
                aw = a * w_recv[s, rows, cols].astype(f32)
                for k in range(CLUSTERS):
                    member = mask[zl * 8 + s, k]
                    nums[k] = nums[k] + member * aw
                    dens[k] = dens[k] + member * a
            for k in range(CLUSTERS):
                num[k, rows, cols] = nums[k]
                den[k, rows, cols] = dens[k]
            return 0

        lax.fori_loop(0, HALF // 256, tile, 0)

    def columns(way, h):
        return pl.ds(pl.multiple_of(h * HALF + way * QUART, QUART), QUART)

    def m_copy(way, j, peer):
        return rcopy(m_send.at[way, j], m_recv.at[way, j], c_s.at[way, j, 0], c_r.at[way, j, 0], peer)

    def d_copy(way, j, peer):
        return rcopy(d_send.at[way, j], d_recv.at[way, j], c_s.at[way, j, 1], c_r.at[way, j, 1], peer)

    def b_copy(way, j, peer):
        rows, _, h = where(j)
        part = merged.at[:, rows, columns(way, h)]
        return rcopy(part, part, b_s.at[way, j], b_r.at[way, j], peer)

    def ends(way):
        if way == 0:
            return zl, line((zl + 1) % 4), line((zl + 3) % 4)
        return 3 - zl, line((zl + 3) % 4), line((zl + 1) % 4)

    def chain(way, i):
        hop, ahead, behind = ends(way)
        j = i - hop

        @pl.when((j >= 0) & (j < NS))
        def _():
            rows, _, h = where(j)
            cols = columns(way, h)

            @pl.when(hop > 0)
            def _():
                m_copy(way, j, behind).wait_recv()
                d_copy(way, j, behind).wait_recv()
                for k in range(CLUSTERS):
                    d = d_recv[way, j, k].astype(f32)
                    v = m_recv[way, j, k].astype(jnp.int32).astype(f32) * (1.0 / CODE)
                    num[k, rows, cols] += v * d
                    den[k, rows, cols] += d

            @pl.when(hop < 3)
            def _():
                for k in range(CLUSTERS):
                    d = den[k, rows, cols]
                    v = num[k, rows, cols] / jnp.maximum(d, 0.0625)
                    m_send[way, j, k] = jnp.round(v * CODE).astype(jnp.int32).astype(jnp.int16)
                    d_send[way, j, k] = d.astype(bf16)
                m_copy(way, j, ahead).start()
                d_copy(way, j, ahead).start()

            @pl.when(hop == 3)
            def _():
                for k in range(CLUSTERS):
                    merged[k, rows, cols] = (num[k, rows, cols] / den[k, rows, cols]).astype(bf16)
                b_copy(way, j, behind).start()

    def back(way, i):
        hop, ahead, behind = ends(way)
        j = i - (6 - hop)

        @pl.when((j >= 0) & (j < NS) & (hop < 3))
        def _():
            b_copy(way, j, ahead).wait_recv()

            @pl.when(hop > 0)
            def _():
                b_copy(way, j, behind).start()

    def o_copy(j, k, owner):
        rows, r, h = where(j)
        cols = pl.ds(pl.multiple_of(h * HALF, HALF), HALF)
        dst = out.at[pl.ds(pl.multiple_of(owner * OWN + r * 16, 16), 16), cols]
        return rcopy(picked.at[k, rows, cols], dst, o_s.at[k, j], o_r.at[owner, j], plane(k))

    def l_copy(j):
        rows, r, h = where(j)
        cols = pl.ds(pl.multiple_of(h * HALF, HALF), HALF)
        dst = out.at[pl.ds(pl.multiple_of(q * OWN + r * 16, 16), 16), cols]
        return pltpu.make_async_copy(picked.at[q, rows, cols], dst, l_s.at[j])

    def scatter(j):
        rows, _, h = where(j)
        cols = pl.ds(pl.multiple_of(h * HALF, HALF), HALF)
        for k in range(8):
            peer = (q + k) % 8
            own_cluster = cluster[zl * 8 + peer, 0]
            v = merged[0, rows, cols]
            for n in range(1, CLUSTERS):
                v = jnp.where(own_cluster == n, merged[n, rows, cols], v)
            picked[peer, rows, cols] = v
            if k == 0:
                l_copy(j).start()
            else:
                o_copy(j, peer, q).start()

    def merge_step(i, _):
        pl.when(i < NS)(lambda: own_sums(i))
        chain(0, i)
        chain(1, i)
        back(0, i)
        back(1, i)
        pl.when(i >= 6)(lambda: scatter(i - 6))
        return 0

    lax.fori_loop(0, NS + 6, merge_step, 0)

    def last_out(j, _):
        l_copy(j).wait()
        for k in range(1, 8):
            peer = (q + k) % 8
            o_copy(j, peer, peer).wait_recv()
            o_copy(j, peer, q).wait_send()
        for way in range(2):
            hop, ahead, behind = ends(way)

            @pl.when(hop < 3)
            def _():
                m_copy(way, j, ahead).wait_send()
                d_copy(way, j, ahead).wait_send()

            @pl.when(hop > 0)
            def _():
                b_copy(way, j, behind).wait_send()
        return 0

    lax.fori_loop(0, NS, last_out, 0)

    def last_a(r, _):
        for k in range(1, 8):
            a_copy(r, (q + k) % 8, q).wait_send()
        return 0

    lax.fori_loop(0, NG, last_a, 0)
    for k in range(1, 8):
        w_copy((q + k) % 8, q).wait_send()
        t_copy((m + k) % 8, m).wait_send()

    def last_mp(b, _):
        for k in range(1, 4):
            y_copy(b, (xx + k) % 4, xx).wait_send()
            xg_copy(b, (xx + k) % 4, xx).wait_send()
        z_copy(b).wait_send()
        zg_copy(b, mine).wait_send()
        return 0

    lax.fori_loop(0, NB, last_mp, 0)


def body(hidden, weight, target, router_prob, routes, assign):
    token_weight = jnp.where(jnp.any(routes[0] == 0, axis=-1), router_prob[0], 0.0)
    token_weight = jnp.broadcast_to(token_weight[:, :, None], (NB, 16, 128))
    member = (assign == jnp.arange(CLUSTERS)[None, :]).astype(f32)
    vmem = pl.BlockSpec(memory_space=pltpu.VMEM)
    smem = pl.BlockSpec(memory_space=pltpu.SMEM)
    V, S = pltpu.VMEM, pltpu.SemaphoreType.DMA
    result = pl.pallas_call(
        kernel,
        out_shape=jax.ShapeDtypeStruct((F, D), bf16),
        in_specs=[vmem, vmem, vmem, vmem, smem, smem],
        out_specs=pl.BlockSpec(memory_space=pl.ANY),
        scratch_shapes=[
            V((NB, F, TOK), bf16),
            V((TOK, D), f32),
            V((NB, 32, D), f32),
            V((NB, TOK, D), bf16),
            V((NB, 4, 32, D), bf16),
            V((NB, 16, D), bf16),
            V((NB, 16, D), bf16),
            V((NB, TOK, D), bf16),
            V((F, D), f32),
            V((8, 8, 256), f32),
            V((F, D), bf16),
            V((8, OWN, D), bf16),
            V((8, OWN, D), bf16),
            V((CLUSTERS, OWN, D), f32),
            V((CLUSTERS, OWN, D), f32),
            V((2, NS, CLUSTERS, G16, QUART), jnp.int16),
            V((2, NS, CLUSTERS, G16, QUART), bf16),
            V((2, NS, CLUSTERS, G16, QUART), jnp.int16),
            V((2, NS, CLUSTERS, G16, QUART), bf16),
            V((CLUSTERS, OWN, D), bf16),
            V((8, OWN, D), bf16),
            S((8,)), S((8,)),
            S((NB, 4)), S((NB, 4)),
            S((NB,)), S((NB,)),
            S((NB,)), S((NB,)),
            S((NB, 4)), S((NB, 4)),
            S((8,)), S((8,)),
            S((8, NG)), S((8, NG)),
            S((2, NS, 2)), S((2, NS, 2)),
            S((2, NS)), S((2, NS)),
            S((8, NS)), S((8, NS)),
            S((NS,)),
        ],
        compiler_params=pltpu.CompilerParams(
            collective_id=0, has_side_effects=True, vmem_limit_bytes=62 << 20
        ),
        cost_estimate=pl.CostEstimate(flops=4_000_000_000, bytes_accessed=12_000_000, transcendentals=0),
    )(hidden[0], weight[0], target[0], token_weight, member, assign)
    return result[None]


def solution(mesh):
    placed = (
        P("client", None, None, "mp"),
        P("client", "mp", None),
        P("client", None, "mp", None),
        P("client", None, "mp"),
        P("client", None, "mp", None),
        P(),
    )
    return jax.shard_map(
        body, mesh=mesh, in_specs=placed, out_specs=P("client", "mp", None), check_vma=False
    )
```

```python
import functools

import jax
import jax.numpy as jnp
from jax import lax
from jax.experimental import pallas as pl
from jax.experimental.pallas import tpu as pltpu
from jax.sharding import PartitionSpec as P

D = 2048
FFW = 7168
NB = 4
CLUSTERS = 4
EPS = 1e-06
FLOOR = 0.1

F = 896
TOK = 128
OWN = 112
G16 = 16
NG = OWN // G16
SPLIT = 4
NS = SPLIT * NG
WIDE = D // SPLIT
HALF = WIDE // 2
LAG = 2
QUART = D // 4
WMAX = 0.0625
CODE = 32760.0 / WMAX
LOW = 0.0625
MID = 9.0
STEP = 11.8 / 32760.0

MESH = pl.DeviceIdType.MESH
f32 = jnp.float32
bf16 = jnp.bfloat16


def rcopy(src, dst, send, recv, device):
    return pltpu.make_async_remote_copy(
        src_ref=src, dst_ref=dst, send_sem=send, recv_sem=recv, device_id=device, device_id_type=MESH
    )


def kernel(
    hid_in, w_in, tgt, prob, routes, cluster, out,
    hid, w, tw, hid_t, y_f32, own, y_send, y_recv, z_send, z_recv, grad_out, fisher, sums, a_send, a_recv, w_recv,
    num, den, c_send, c_recv, merged, picked,
    in_s, w_s, w_r, y_s, y_r, z_s, z_r, zg_s, zg_r, xg_s, xg_r, t_s, t_r, a_s, a_r, c_s, c_r, b_s, b_r, o_s, o_r, l_s,
):
    c = lax.axis_index("client")
    m = lax.axis_index("mp")
    zl, q = c // 8, c % 8
    xx, zh = m // 2, m % 2

    def plane(k):
        return (zl * 8 + k, m)

    def group(k):
        return (c, k)

    def line(k):
        return (k * 8 + q, m)

    barrier = pltpu.get_barrier_semaphore()
    for k in range(1, 8):
        pl.semaphore_signal(barrier, inc=1, device_id=plane((q + k) % 8), device_id_type=MESH)
        pl.semaphore_signal(barrier, inc=1, device_id=group((m + k) % 8), device_id_type=MESH)

    for k in (1, 3):
        pl.semaphore_signal(barrier, inc=1, device_id=line((zl + k) % 4), device_id_type=MESH)
    load_hid = pltpu.make_async_copy(hid_in, hid, in_s.at[0])
    load_w = pltpu.make_async_copy(w_in, w, in_s.at[1])
    load_hid.start()
    load_w.start()

    eye = lax.broadcasted_iota(jnp.int32, (16, 16), 0) == lax.broadcasted_iota(jnp.int32, (16, 16), 1)
    for b in range(NB):
        chosen = jnp.max(jnp.where(routes[b] == 0, 1.0, 0.0), axis=0, keepdims=True) > 0
        row = jnp.where(chosen, prob[b : b + 1, :], 0.0)
        column = jnp.sum(jnp.where(eye, jnp.broadcast_to(row, (16, 16)), 0.0), axis=1, keepdims=True)
        tw[b] = jnp.broadcast_to(column, (16, 128))
    load_hid.wait()
    load_w.wait()

    def w_copy(k, slot):
        rows = pl.ds(pl.multiple_of(k * OWN, 16), OWN)
        return rcopy(w.at[rows], w_recv.at[slot], w_s.at[k], w_r.at[slot], plane(k))

    def y_copy(b, k, slot):
        rows = pl.ds(pl.multiple_of(k * 32, 32), 32)
        return rcopy(
            y_send.at[b, rows], y_recv.at[b, slot], y_s.at[b, k], y_r.at[b, slot], group(k * 2 + zh)
        )

    def y_batch(b, _):
        for n in range(4):
            cols = pl.ds(n * QUART, QUART)
            y_f32[:, cols] = jnp.dot(hid[b], w[:, cols], preferred_element_type=f32)
            y_send[b, :, cols] = y_f32[:, cols].astype(bf16)
        own[b] = y_f32[pl.ds(pl.multiple_of(xx * 32, 32), 32), :]

        @pl.when(b == 0)
        def _():
            pl.semaphore_wait(barrier, 16)

        for k in range(1, 4):
            y_copy(b, (xx + k) % 4, xx).start()
        return 0

    lax.fori_loop(0, NB, y_batch, 0)

    for k in range(1, 8):
        w_copy((q + k) % 8, q).start()

    def prepare(b, _):
        hid_t[b] = hid[b].T
        return 0

    lax.fori_loop(0, NB, prepare, 0)

    def clear(r, _):
        rows = pl.ds(pl.multiple_of(r * 16, 16), 16)
        fisher[rows] = jnp.zeros((16, D), f32)
        return 0

    lax.fori_loop(0, F // 16, clear, 0)
    sums[m] = jnp.zeros((8, 256), f32)

    def keep_w(r, _):
        w_recv[q, pl.ds(pl.multiple_of(r * 16, 16), 16)] = w[pl.ds(pl.multiple_of(q * OWN + r * 16, 16), 16)]
        return 0

    lax.fori_loop(0, NG, keep_w, 0)

    mine = pl.ds(pl.multiple_of(m * 16, 16), 16)
    theirs = pl.ds(pl.multiple_of((xx * 2 + 1 - zh) * 16, 16), 16)
    partner = group(xx * 2 + 1 - zh)

    def z_copy(b):
        return rcopy(z_send.at[b], z_recv.at[b], z_s.at[b], z_r.at[b], partner)

    def zg_copy(b, rows):
        return rcopy(grad_out.at[b, rows], grad_out.at[b, rows], zg_s.at[b], zg_r.at[b], partner)

    def xg_copy(b, k, block):
        rows = pl.ds(pl.multiple_of(block * 32, 32), 32)
        return rcopy(
            grad_out.at[b, rows], grad_out.at[b, rows], xg_s.at[b, k], xg_r.at[b, block], group(k * 2 + zh)
        )

    def step_x(b):
        total = own[b]
        for k in range(1, 4):
            slot = (xx + k) % 4
            y_copy(b, slot, slot).wait_recv()
            total = total + y_recv[b, slot].astype(f32)
        own[b] = total
        z_send[b] = own[b, pl.ds(pl.multiple_of((1 - zh) * 16, 16), 16)].astype(bf16)
        z_copy(b).start()

    def step_z(b):
        z_copy(b).wait_recv()
        y = own[b, pl.ds(pl.multiple_of(zh * 16, 16), 16)] + z_recv[b].astype(f32)
        grad_out[b, mine] = (tw[b][:, :1] * (y - tgt[b].astype(f32))).astype(bf16)
        zg_copy(b, mine).start()

    def step_g(b):
        zg_copy(b, theirs).wait_recv()
        for k in range(1, 4):
            xg_copy(b, (xx + k) % 4, xx).start()

    def step_f(b):
        for k in range(1, 4):
            slot = (xx + k) % 4
            xg_copy(b, slot, slot).wait_recv()

        def tile(n, _):
            cols = pl.ds(pl.multiple_of(n * 256, 256), 256)
            g = jnp.dot(hid_t[b], grad_out[b, :, cols], preferred_element_type=f32)
            g = g * g
            fisher[:, cols] += g
            sums[m] += g.reshape(F // 8, 8, 256).sum(0)
            return 0

        lax.fori_loop(0, D // 256, tile, 0)

    def mp_step(t, _):
        pl.when(t < NB)(lambda: step_x(t))
        pl.when((t >= 1) & (t < NB + 1))(lambda: step_z(t - 1))
        pl.when((t >= 2) & (t < NB + 2))(lambda: step_g(t - 2))
        pl.when(t >= 3)(lambda: step_f(t - 3))
        return 0

    lax.fori_loop(0, NB + 3, mp_step, 0)

    def t_copy(k, slot):
        return rcopy(sums.at[slot], sums.at[slot], t_s.at[k], t_r.at[slot], group(k))

    for k in range(1, 8):
        t_copy((m + k) % 8, m).start()
    for k in range(1, 8):
        slot = (m + k) % 8
        t_copy(slot, slot).wait_recv()
    total = sums[0]
    for k in range(1, 8):
        total = total + sums[k]
    mean = jnp.sum(total) / (FFW * D)
    scale = 1.0 / jnp.full((8, 128), mean + EPS, f32)
    scale = scale[:1, :1]

    def a_copy(r, k, slot):
        src = pl.ds(pl.multiple_of(k * OWN + r * 16, 16), 16)
        dst = pl.ds(pl.multiple_of(r * 16, 16), 16)
        return rcopy(a_send.at[src], a_recv.at[slot, dst], a_s.at[k], a_r.at[slot, r], plane(k))

    def a_group(r, _):
        for k in range(1, 8):
            peer = (q + k) % 8
            rows = pl.ds(pl.multiple_of(peer * OWN + r * 16, 16), 16)
            a_send[rows] = (fisher[rows] * scale + FLOOR).astype(bf16)
            a_copy(r, peer, q).start()
        rows = pl.ds(pl.multiple_of(q * OWN + r * 16, 16), 16)
        a_recv[q, pl.ds(pl.multiple_of(r * 16, 16), 16)] = (fisher[rows] * scale + FLOOR).astype(bf16)
        return 0

    lax.fori_loop(0, NG, a_group, 0)

    for k in range(1, 8):
        slot = (q + k) % 8
        w_copy(slot, slot).wait_recv()

    def where(j):
        r, h = j // SPLIT, j % SPLIT
        return pl.ds(pl.multiple_of(r * 16, 16), 16), r, h

    def own_sums(j):
        rows, r, h = where(j)

        @pl.when(h == 0)
        def _():
            for k in range(1, 8):
                slot = (q + k) % 8
                a_copy(r, slot, slot).wait_recv()

        belongs = [cluster[0, zl * 8 + s] for s in range(8)]
        for n in range(WIDE // 256):
            cols = pl.ds(pl.multiple_of(h * WIDE + n * 256, 256), 256)
            nums = [jnp.zeros((16, 256), f32)] * CLUSTERS
            dens = [jnp.zeros((16, 256), f32)] * CLUSTERS
            for s in range(8):
                a = a_recv[s, rows, cols].astype(f32)
                aw = a * w_recv[s, rows, cols].astype(f32)
                for k in range(CLUSTERS):
                    member = jnp.where(belongs[s] == k, 1.0, 0.0)
                    nums[k] = nums[k] + member * aw
                    dens[k] = dens[k] + member * a
            for k in range(CLUSTERS):
                num[k, rows, cols] = nums[k]
                den[k, rows, cols] = dens[k]

    def columns(way, h):
        return pl.ds(pl.multiple_of(h * WIDE + way * HALF, HALF), HALF)

    def c_copy(way, j, peer):
        return rcopy(c_send.at[way, j], c_recv.at[way, j], c_s.at[way], c_r.at[way, j], peer)

    def b_copy(way, j, peer):
        rows, _, h = where(j)
        part = merged.at[:, rows, columns(way, h)]
        return rcopy(part, part, b_s.at[way], b_r.at[way, j], peer)

    def ends(way):
        if way == 0:
            return zl, line((zl + 1) % 4), line((zl + 3) % 4)
        return 3 - zl, line((zl + 3) % 4), line((zl + 1) % 4)

    def chain(way, i):
        hop, ahead, behind = ends(way)
        j = i - LAG * hop

        @pl.when((j >= 0) & (j < NS))
        def _():
            rows, _, h = where(j)
            cols = columns(way, h)

            @pl.when(hop > 0)
            def _():
                c_copy(way, j, behind).wait_recv()
                for k in range(CLUSTERS):
                    v = c_recv[way, j, k].astype(jnp.int32).astype(f32) * (1.0 / CODE)
                    e = c_recv[way, j, CLUSTERS + k].astype(jnp.int32)
                    d = jnp.where(e < -32000, 0.0, jnp.exp(e.astype(f32) * STEP + MID))
                    num[k, rows, cols] += v * d
                    den[k, rows, cols] += d

            @pl.when(hop < 3)
            def _():
                for k in range(CLUSTERS):
                    d = jnp.maximum(den[k, rows, cols], LOW)
                    v = num[k, rows, cols] / d
                    e = (jnp.log(d) - MID) * (1.0 / STEP)
                    c_send[way, j, k] = jnp.round(v * CODE).astype(jnp.int32).astype(jnp.int16)
                    c_send[way, j, CLUSTERS + k] = jnp.round(e).astype(jnp.int32).astype(jnp.int16)
                c_copy(way, j, ahead).start()

            @pl.when(hop == 3)
            def _():
                for k in range(CLUSTERS):
                    merged[k, rows, cols] = (num[k, rows, cols] / den[k, rows, cols]).astype(bf16)
                b_copy(way, j, behind).start()

    def back(way, i):
        hop, ahead, behind = ends(way)
        j = i - LAG * (6 - hop)

        @pl.when((j >= 0) & (j < NS) & (hop < 3))
        def _():
            b_copy(way, j, ahead).wait_recv()

            @pl.when(hop > 0)
            def _():
                b_copy(way, j, behind).start()

    def o_copy(j, k, owner):
        rows, r, h = where(j)
        cols = pl.ds(pl.multiple_of(h * WIDE, WIDE), WIDE)
        dst = out.at[pl.ds(pl.multiple_of(owner * OWN + r * 16, 16), 16), cols]
        return rcopy(picked.at[k, rows, cols], dst, o_s.at[k], o_r.at[owner], plane(k))

    def o_all(k, owner):
        dst = out.at[pl.ds(pl.multiple_of(owner * OWN, 16), OWN)]
        return rcopy(picked.at[k], dst, o_s.at[k], o_r.at[owner], plane(k))

    def l_copy(j):
        rows, r, h = where(j)
        cols = pl.ds(pl.multiple_of(h * WIDE, WIDE), WIDE)
        dst = out.at[pl.ds(pl.multiple_of(q * OWN + r * 16, 16), 16), cols]
        return pltpu.make_async_copy(picked.at[q, rows, cols], dst, l_s.at[0])

    def scatter(j):
        rows, _, h = where(j)
        cols = pl.ds(pl.multiple_of(h * WIDE, WIDE), WIDE)
        for k in range(8):
            peer = (q + k) % 8
            own_cluster = cluster[0, zl * 8 + peer]
            v = merged[0, rows, cols]
            for n in range(1, CLUSTERS):
                v = jnp.where(own_cluster == n, merged[n, rows, cols], v)
            picked[peer, rows, cols] = v
            if k == 0:
                l_copy(j).start()
            else:
                o_copy(j, peer, q).start()

    own_sums(0)

    def merge_step(i, _):
        chain(0, i)
        chain(1, i)
        back(0, i)
        back(1, i)
        pl.when(i >= 6 * LAG)(lambda: scatter(i - 6 * LAG))
        pl.when(i + 1 < NS)(lambda: own_sums(i + 1))
        return 0

    lax.fori_loop(0, NS + 6 * LAG, merge_step, 0)

    for k in range(1, 8):
        peer = (q + k) % 8
        o_all(peer, peer).wait_recv()
        o_all(peer, q).wait_send()
        rcopy(a_send.at[pl.ds(pl.multiple_of(peer * OWN, 16), OWN)], a_recv.at[q], a_s.at[peer], a_r.at[q, 0], plane(peer)).wait_send()
        w_copy(peer, q).wait_send()
        t_copy((m + k) % 8, m).wait_send()
    pltpu.make_async_copy(picked.at[q], out.at[pl.ds(pl.multiple_of(q * OWN, 16), OWN)], l_s.at[0]).wait()
    for way in range(2):
        hop, ahead, behind = ends(way)

        @pl.when(hop < 3)
        def _():
            rcopy(c_send.at[way], c_recv.at[way], c_s.at[way], c_r.at[way, 0], ahead).wait_send()

        @pl.when(hop > 0)
        def _():
            part = merged.at[:, :, pl.ds(way * (D // 2), D // 2)]
            rcopy(part, part, b_s.at[way], b_r.at[way, 0], behind).wait_send()

    def last_mp(b, _):
        for k in range(1, 4):
            y_copy(b, (xx + k) % 4, xx).wait_send()
            xg_copy(b, (xx + k) % 4, xx).wait_send()
        z_copy(b).wait_send()
        zg_copy(b, mine).wait_send()
        return 0

    lax.fori_loop(0, NB, last_mp, 0)


def body(hidden, weight, target, router_prob, routes, assign):
    vmem = pl.BlockSpec(memory_space=pltpu.VMEM)
    smem = pl.BlockSpec(memory_space=pltpu.SMEM)
    hbm = pl.BlockSpec(memory_space=pl.ANY)
    V, S = pltpu.VMEM, pltpu.SemaphoreType.DMA
    result = pl.pallas_call(
        kernel,
        out_shape=jax.ShapeDtypeStruct((F, D), bf16),
        in_specs=[hbm, hbm, vmem, vmem, vmem, smem],
        out_specs=hbm,
        scratch_shapes=[
            V((NB, TOK, F), bf16),
            V((F, D), bf16),
            V((NB, 16, 128), f32),
            V((NB, F, TOK), bf16),
            V((TOK, D), f32),
            V((NB, 32, D), f32),
            V((NB, TOK, D), bf16),
            V((NB, 4, 32, D), bf16),
            V((NB, 16, D), bf16),
            V((NB, 16, D), bf16),
            V((NB, TOK, D), bf16),
            V((F, D), f32),
            V((8, 8, 256), f32),
            V((F, D), bf16),
            V((8, OWN, D), bf16),
            V((8, OWN, D), bf16),
            V((CLUSTERS, OWN, D), f32),
            V((CLUSTERS, OWN, D), f32),
            V((2, NS, 2 * CLUSTERS, G16, HALF), jnp.int16),
            V((2, NS, 2 * CLUSTERS, G16, HALF), jnp.int16),
            V((CLUSTERS, OWN, D), bf16),
            V((8, OWN, D), bf16),
            S((2,)),
            S((8,)), S((8,)),
            S((NB, 4)), S((NB, 4)),
            S((NB,)), S((NB,)),
            S((NB,)), S((NB,)),
            S((NB, 4)), S((NB, 4)),
            S((8,)), S((8,)),
            S((8,)), S((8, NG)),
            S((2,)), S((2, NS)),
            S((2,)), S((2, NS)),
            S((8,)), S((8,)),
            S((1,)),
        ],
        compiler_params=pltpu.CompilerParams(
            collective_id=0, has_side_effects=True, vmem_limit_bytes=62 << 20
        ),
        cost_estimate=pl.CostEstimate(flops=4_000_000_000, bytes_accessed=12_000_000, transcendentals=0),
    )(hidden[0], weight[0], target[0], router_prob[0], routes[0].transpose(0, 2, 1), assign.reshape(1, -1))
    return result[None]


def solution(mesh):
    placed = (
        P("client", None, None, "mp"),
        P("client", "mp", None),
        P("client", None, "mp", None),
        P("client", None, "mp"),
        P("client", None, "mp", None),
        P(),
    )
    return jax.shard_map(
        body, mesh=mesh, in_specs=placed, out_specs=P("client", "mp", None), check_vma=False
    )
```

```python
import functools

import jax
import jax.numpy as jnp
from jax import lax
from jax.experimental import pallas as pl
from jax.experimental.pallas import tpu as pltpu
from jax.sharding import PartitionSpec as P

D = 2048
FFW = 7168
NB = 4
CLUSTERS = 4
EPS = 1e-06
FLOOR = 0.1

F = 896
TOK = 128
OWN = 112
G16 = 16
NG = OWN // G16
SPLIT = 4
NS = SPLIT * NG
WIDE = D // SPLIT
HALF = WIDE // 2
LAG = 2
QUART = D // 4
WMAX = 0.0625
CODE = 32760.0 / WMAX
LOW = 0.0625
MID = 9.0
STEP = 11.8 / 32760.0

MESH = pl.DeviceIdType.MESH
f32 = jnp.float32
bf16 = jnp.bfloat16


def rcopy(src, dst, send, recv, device):
    return pltpu.make_async_remote_copy(
        src_ref=src, dst_ref=dst, send_sem=send, recv_sem=recv, device_id=device, device_id_type=MESH
    )


def kernel(
    hid_in, w_in, tgt, prob, routes, cluster, out,
    hid, w, tw, hid_t, y_all, y_send, y_half, y_full, z_send, z_recv, grad_out, fisher, gram, sums, a_send, a_recv, w_recv,
    num, den, c_send, c_recv, merged, picked,
    in_s, w_s, w_r, yh_s, yh_r, yf_s, yf_r, z_s, z_r, zg_s, zg_r, xg_s, xg_r, xh_s, xh_r, t_s, t_r, a_s, a_r, f_r, c_s, c_r, b_s, b_r, o_s, o_r, l_s,
):
    c = lax.axis_index("client")
    m = lax.axis_index("mp")
    zl, q = c // 8, c % 8
    xx, zh = m // 2, m % 2

    def plane(k):
        return (zl * 8 + k, m)

    def group(k):
        return (c, k)

    def line(k):
        return (k * 8 + q, m)

    barrier = pltpu.get_barrier_semaphore()
    for k in range(1, 8):
        pl.semaphore_signal(barrier, inc=1, device_id=plane((q + k) % 8), device_id_type=MESH)
        pl.semaphore_signal(barrier, inc=1, device_id=group((m + k) % 8), device_id_type=MESH)

    for k in (1, 3):
        pl.semaphore_signal(barrier, inc=1, device_id=line((zl + k) % 4), device_id_type=MESH)
    load_hid = pltpu.make_async_copy(hid_in, hid, in_s.at[0])
    load_w = pltpu.make_async_copy(w_in, w, in_s.at[1])
    load_hid.start()
    load_w.start()

    eye = lax.broadcasted_iota(jnp.int32, (16, 16), 0) == lax.broadcasted_iota(jnp.int32, (16, 16), 1)
    for b in range(NB):
        chosen = jnp.max(jnp.where(routes[b] == 0, 1.0, 0.0), axis=0, keepdims=True) > 0
        row = jnp.where(chosen, prob[b : b + 1, :], 0.0)
        column = jnp.sum(jnp.where(eye, jnp.broadcast_to(row, (16, 16)), 0.0), axis=1, keepdims=True)
        tw[b] = jnp.broadcast_to(column, (16, 128))
    load_hid.wait()
    load_w.wait()

    def w_copy(k, slot):
        rows = pl.ds(pl.multiple_of(k * OWN, 16), OWN)
        return rcopy(w.at[rows], w_recv.at[slot], w_s.at[k], w_r.at[slot], plane(k))

    right, left, opposite = (xx + 1) % 4, (xx + 3) % 4, (xx + 2) % 4
    side = [group(right * 2 + zh), group(left * 2 + zh)]

    def block(k):
        return pl.ds(pl.multiple_of(k * 32, 32), 32)

    def half(k, h):
        return pl.ds(pl.multiple_of(k * 32 + h * 16, 16), 16)

    def yh_copy(b, h):
        return rcopy(y_send.at[b, half(opposite, h)], y_half.at[b, h], yh_s.at[b, h], yh_r.at[b, h], side[h])

    def yf_copy(b, h):
        return rcopy(
            y_send.at[b, block((right, left)[h])], y_full.at[b, h], yf_s.at[b, h], yf_r.at[b, h], side[h]
        )

    def step_y(b):
        for n in range(4):
            cols = pl.ds(n * QUART, QUART)
            y_all[b, :, cols] = jnp.dot(hid[b], w[:, cols], preferred_element_type=f32)
        y_send[b, block(opposite)] = y_all[b, block(opposite)].astype(bf16)

        @pl.when(b == 0)
        def _():
            pl.semaphore_wait(barrier, 16)

        for h in range(2):
            yh_copy(b, h).start()

    def step_r(b):
        for h in range(2):
            k = (right, left)[h]
            y_send[b, half(k, 1 - h)] = y_all[b, half(k, 1 - h)].astype(bf16)
            yh_copy(b, h).wait_recv()
            y_send[b, half(k, h)] = (y_all[b, half(k, h)] + y_half[b, h].astype(f32)).astype(bf16)
            yf_copy(b, h).start()

    def prepare(b):
        hid_t[b] = hid[b].T
        gram[b] = lax.dot_general(hid[b], hid[b], (((1,), (1,)), ((), ())), preferred_element_type=f32)
        fisher[pl.ds(pl.multiple_of(b * (F // NB), 32), F // NB)] = jnp.zeros((F // NB, D), f32)

        @pl.when(b == 0)
        def _():
            sums[m] = jnp.zeros((8, 128), f32)
            for k in range(1, 8):
                w_copy((q + k) % 8, q).start()

        @pl.when(b == 1)
        def _():
            w_recv[q] = w[pl.ds(pl.multiple_of(q * OWN, 16), OWN)]

    mine = pl.ds(pl.multiple_of(m * 16, 16), 16)
    theirs = pl.ds(pl.multiple_of((xx * 2 + 1 - zh) * 16, 16), 16)
    partner = group(xx * 2 + 1 - zh)

    def z_copy(b):
        return rcopy(z_send.at[b], z_recv.at[b], z_s.at[b], z_r.at[b], partner)

    def zg_copy(b, rows):
        return rcopy(grad_out.at[b, rows], grad_out.at[b, rows], zg_s.at[b], zg_r.at[b], partner)

    def xg_copy(b, h, k):
        part = grad_out.at[b, block(k)]
        return rcopy(part, part, xg_s.at[b, h], xg_r.at[b, h], side[h])

    def xh_copy(b, h, k):
        part = grad_out.at[b, half(k, h)]
        return rcopy(part, part, xh_s.at[b, h], xh_r.at[b, h], side[h])

    def step_x(b):
        for h in range(2):
            yf_copy(b, h).wait_recv()
        z_send[b] = (
            y_all[b, theirs] + y_full[b, 0, half(0, 1 - zh)].astype(f32) + y_full[b, 1, half(0, 1 - zh)].astype(f32)
        ).astype(bf16)
        z_copy(b).start()

    def step_z(b):
        y = y_all[b, mine] + y_full[b, 0, half(0, zh)].astype(f32) + y_full[b, 1, half(0, zh)].astype(f32)
        z_copy(b).wait_recv()
        y = y + z_recv[b].astype(f32)
        grad_out[b, mine] = (tw[b][:, :1] * (y - tgt[b].astype(f32))).astype(bf16)
        zg_copy(b, mine).start()

    def step_g(b):
        zg_copy(b, theirs).wait_recv()
        for h in range(2):
            xg_copy(b, h, xx).start()

    def step_h(b):
        for h in range(2):
            k = (left, right)[h]
            xg_copy(b, h, k).wait_recv()
            xh_copy(b, h, k).start()

    def t_copy(k, slot):
        return rcopy(sums.at[slot], sums.at[slot], t_s.at[k], t_r.at[slot], group(k))

    def step_f(b):
        for h in range(2):
            xh_copy(b, h, opposite).wait_recv()
        tokens = lax.dot_general(
            grad_out[b], grad_out[b], (((1,), (1,)), ((), ())), preferred_element_type=f32
        )
        sums[m] += (tokens * gram[b]).reshape(TOK // 8, 8, TOK).sum(0)

        @pl.when(b == NB - 1)
        def _():
            for k in range(1, 8):
                t_copy((m + k) % 8, m).start()

        def tile(n, _):
            cols = pl.ds(pl.multiple_of(n * 256, 256), 256)
            g = jnp.dot(hid_t[b], grad_out[b, :, cols], preferred_element_type=f32)
            fisher[:, cols] += g * g
            return 0

        lax.fori_loop(0, D // 256, tile, 0)

    def mp_step(t, _):
        pl.when(t < NB)(lambda: step_y(t))
        pl.when((t >= 1) & (t < NB + 1))(lambda: step_r(t - 1))
        pl.when((t >= 2) & (t < NB + 2))(lambda: step_x(t - 2))
        pl.when((t >= 3) & (t < NB + 3))(lambda: step_z(t - 3))
        pl.when((t >= 4) & (t < NB + 4))(lambda: step_g(t - 4))
        pl.when((t >= 5) & (t < NB + 5))(lambda: step_h(t - 5))
        pl.when(t < NB)(lambda: prepare(t))
        pl.when(t >= 6)(lambda: step_f(t - 6))
        return 0

    lax.fori_loop(0, NB + 6, mp_step, 0)

    for k in range(1, 8):
        slot = (m + k) % 8
        t_copy(slot, slot).wait_recv()
    total = sums[0]
    for k in range(1, 8):
        total = total + sums[k]
    mean = jnp.sum(total) / (FFW * D)
    scale = 1.0 / jnp.full((8, 128), mean + EPS, f32)
    scale = scale[:1, :1]

    def a_copy(r, k, slot):
        src = pl.ds(pl.multiple_of(k * OWN + r * 16, 16), 16)
        dst = pl.ds(pl.multiple_of(r * 16, 16), 16)
        return rcopy(a_send.at[src], a_recv.at[slot, dst], a_s.at[k], a_r.at[slot, r], plane(k))

    def a_group(r):
        for k in range(1, 8):
            peer = (q + k) % 8
            rows = pl.ds(pl.multiple_of(peer * OWN + r * 16, 16), 16)
            a_send[rows] = (fisher[rows] * scale + FLOOR).astype(bf16)
            a_copy(r, peer, q).start()
        rows = pl.ds(pl.multiple_of(q * OWN + r * 16, 16), 16)
        a_recv[q, pl.ds(pl.multiple_of(r * 16, 16), 16)] = (fisher[rows] * scale + FLOOR).astype(bf16)

    def f_copy(h, k, slot):
        cols = pl.ds(h * WIDE, WIDE)
        src = a_send.at[pl.ds(pl.multiple_of(k * OWN, 16), 16), cols]
        return rcopy(src, a_recv.at[slot, pl.ds(0, 16), cols], a_s.at[k], f_r.at[slot, h], plane(k))

    for h in range(SPLIT):
        cols = pl.ds(h * WIDE, WIDE)
        for k in range(1, 8):
            peer = (q + k) % 8
            rows = pl.ds(pl.multiple_of(peer * OWN, 16), 16)
            a_send[rows, cols] = (fisher[rows, cols] * scale + FLOOR).astype(bf16)
            f_copy(h, peer, q).start()
        a_recv[q, :16, cols] = (fisher[pl.ds(pl.multiple_of(q * OWN, 16), 16), cols] * scale + FLOOR).astype(bf16)

    for k in range(1, 8):
        slot = (q + k) % 8
        w_copy(slot, slot).wait_recv()

    def where(j):
        r, h = j // SPLIT, j % SPLIT
        return pl.ds(pl.multiple_of(r * 16, 16), 16), r, h

    def own_sums(j):
        rows, r, h = where(j)

        for piece in range(SPLIT):

            @pl.when(j == piece)
            def _():
                for k in range(1, 8):
                    slot = (q + k) % 8
                    f_copy(piece, slot, slot).wait_recv()

        @pl.when((h == 0) & (r > 0))
        def _():
            for k in range(1, 8):
                slot = (q + k) % 8
                a_copy(r, slot, slot).wait_recv()

        belongs = [cluster[0, zl * 8 + s] for s in range(8)]
        for n in range(WIDE // 256):
            cols = pl.ds(pl.multiple_of(h * WIDE + n * 256, 256), 256)
            nums = [jnp.zeros((16, 256), f32)] * CLUSTERS
            dens = [jnp.zeros((16, 256), f32)] * CLUSTERS
            for s in range(8):
                a = a_recv[s, rows, cols].astype(f32)
                aw = a * w_recv[s, rows, cols].astype(f32)
                for k in range(CLUSTERS):
                    member = jnp.where(belongs[s] == k, 1.0, 0.0)
                    nums[k] = nums[k] + member * aw
                    dens[k] = dens[k] + member * a
            for k in range(CLUSTERS):
                num[k, rows, cols] = nums[k]
                den[k, rows, cols] = dens[k]

    def columns(way, h):
        return pl.ds(pl.multiple_of(h * WIDE + way * HALF, HALF), HALF)

    def c_copy(way, j, peer):
        return rcopy(c_send.at[way, j], c_recv.at[way, j], c_s.at[way], c_r.at[way, j], peer)

    def b_copy(way, j, peer):
        rows, _, h = where(j)
        part = merged.at[:, rows, columns(way, h)]
        return rcopy(part, part, b_s.at[way], b_r.at[way, j], peer)

    def ends(way):
        if way == 0:
            return zl, line((zl + 1) % 4), line((zl + 3) % 4)
        return 3 - zl, line((zl + 3) % 4), line((zl + 1) % 4)

    def chain(way, i):
        hop, ahead, behind = ends(way)
        j = i - LAG * hop

        @pl.when((j >= 0) & (j < NS))
        def _():
            rows, _, h = where(j)
            cols = columns(way, h)

            @pl.when(hop > 0)
            def _():
                c_copy(way, j, behind).wait_recv()
                for k in range(CLUSTERS):
                    v = c_recv[way, j, k].astype(jnp.int32).astype(f32) * (1.0 / CODE)
                    e = c_recv[way, j, CLUSTERS + k].astype(jnp.int32)
                    d = jnp.where(e < -32000, 0.0, jnp.exp(e.astype(f32) * STEP + MID))
                    num[k, rows, cols] += v * d
                    den[k, rows, cols] += d

            @pl.when(hop < 3)
            def _():
                for k in range(CLUSTERS):
                    d = jnp.maximum(den[k, rows, cols], LOW)
                    v = num[k, rows, cols] / d
                    e = (jnp.log(d) - MID) * (1.0 / STEP)
                    c_send[way, j, k] = jnp.round(v * CODE).astype(jnp.int32).astype(jnp.int16)
                    c_send[way, j, CLUSTERS + k] = jnp.round(e).astype(jnp.int32).astype(jnp.int16)
                c_copy(way, j, ahead).start()

            @pl.when(hop == 3)
            def _():
                for k in range(CLUSTERS):
                    merged[k, rows, cols] = (num[k, rows, cols] / den[k, rows, cols]).astype(bf16)
                b_copy(way, j, behind).start()

    def back(way, i):
        hop, ahead, behind = ends(way)
        j = i - LAG * (6 - hop)

        @pl.when((j >= 0) & (j < NS) & (hop < 3))
        def _():
            b_copy(way, j, ahead).wait_recv()

            @pl.when(hop > 0)
            def _():
                b_copy(way, j, behind).start()

    def o_copy(j, k, owner):
        rows, r, h = where(j)
        cols = pl.ds(pl.multiple_of(h * WIDE, WIDE), WIDE)
        dst = out.at[pl.ds(pl.multiple_of(owner * OWN + r * 16, 16), 16), cols]
        return rcopy(picked.at[k, rows, cols], dst, o_s.at[k], o_r.at[owner], plane(k))

    def o_all(k, owner):
        dst = out.at[pl.ds(pl.multiple_of(owner * OWN, 16), OWN)]
        return rcopy(picked.at[k], dst, o_s.at[k], o_r.at[owner], plane(k))

    def l_copy(j):
        rows, r, h = where(j)
        cols = pl.ds(pl.multiple_of(h * WIDE, WIDE), WIDE)
        dst = out.at[pl.ds(pl.multiple_of(q * OWN + r * 16, 16), 16), cols]
        return pltpu.make_async_copy(picked.at[q, rows, cols], dst, l_s.at[0])

    def scatter(j):
        rows, _, h = where(j)
        cols = pl.ds(pl.multiple_of(h * WIDE, WIDE), WIDE)
        for k in range(8):
            peer = (q + k) % 8
            own_cluster = cluster[0, zl * 8 + peer]
            v = merged[0, rows, cols]
            for n in range(1, CLUSTERS):
                v = jnp.where(own_cluster == n, merged[n, rows, cols], v)
            picked[peer, rows, cols] = v
            if k == 0:
                l_copy(j).start()
            else:
                o_copy(j, peer, q).start()

    a_group(1)
    own_sums(0)

    def merge_step(i, _):
        pl.when((i % SPLIT == 0) & (i // SPLIT + 2 < NG))(lambda: a_group(i // SPLIT + 2))
        chain(0, i)
        chain(1, i)
        back(0, i)
        back(1, i)
        pl.when(i >= 6 * LAG)(lambda: scatter(i - 6 * LAG))
        pl.when(i + 1 < NS)(lambda: own_sums(i + 1))
        return 0

    lax.fori_loop(0, NS + 6 * LAG, merge_step, 0)

    for k in range(1, 8):
        peer = (q + k) % 8
        o_all(peer, peer).wait_recv()
        o_all(peer, q).wait_send()
        rcopy(a_send.at[pl.ds(pl.multiple_of(peer * OWN, 16), OWN)], a_recv.at[q], a_s.at[peer], a_r.at[q, 0], plane(peer)).wait_send()
        w_copy(peer, q).wait_send()
        t_copy((m + k) % 8, m).wait_send()
    pltpu.make_async_copy(picked.at[q], out.at[pl.ds(pl.multiple_of(q * OWN, 16), OWN)], l_s.at[0]).wait()
    for way in range(2):
        hop, ahead, behind = ends(way)

        @pl.when(hop < 3)
        def _():
            rcopy(c_send.at[way], c_recv.at[way], c_s.at[way], c_r.at[way, 0], ahead).wait_send()

        @pl.when(hop > 0)
        def _():
            part = merged.at[:, :, pl.ds(way * (D // 2), D // 2)]
            rcopy(part, part, b_s.at[way], b_r.at[way, 0], behind).wait_send()

    def last_mp(b, _):
        for h in range(2):
            yh_copy(b, h).wait_send()
            yf_copy(b, h).wait_send()
            xg_copy(b, h, xx).wait_send()
            xh_copy(b, h, opposite).wait_send()
        z_copy(b).wait_send()
        zg_copy(b, mine).wait_send()
        return 0

    lax.fori_loop(0, NB, last_mp, 0)


def store(src, dst, sem):
    copy = pltpu.make_async_copy(src, dst, sem.at[0])
    copy.start()
    copy.wait()


def body(hidden, weight, target, router_prob, routes, assign):
    vmem = pl.BlockSpec(memory_space=pltpu.VMEM)
    smem = pl.BlockSpec(memory_space=pltpu.SMEM)
    hbm = pl.BlockSpec(memory_space=pl.ANY)
    V, S = pltpu.VMEM, pltpu.SemaphoreType.DMA
    result = pl.pallas_call(
        kernel,
        out_shape=pltpu.VMEM((F, D), bf16),
        in_specs=[hbm, hbm, vmem, vmem, vmem, smem],
        out_specs=vmem,
        scratch_shapes=[
            V((NB, TOK, F), bf16),
            V((F, D), bf16),
            V((NB, 16, 128), f32),
            V((NB, F, TOK), bf16),
            V((NB, TOK, D), f32),
            V((NB, TOK, D), bf16),
            V((NB, 2, 16, D), bf16),
            V((NB, 2, 32, D), bf16),
            V((NB, 16, D), bf16),
            V((NB, 16, D), bf16),
            V((NB, TOK, D), bf16),
            V((F, D), f32),
            V((NB, TOK, TOK), f32),
            V((8, 8, 128), f32),
            V((F, D), bf16),
            V((8, OWN, D), bf16),
            V((8, OWN, D), bf16),
            V((CLUSTERS, OWN, D), f32),
            V((CLUSTERS, OWN, D), f32),
            V((2, NS, 2 * CLUSTERS, G16, HALF), jnp.int16),
            V((2, NS, 2 * CLUSTERS, G16, HALF), jnp.int16),
            V((CLUSTERS, OWN, D), bf16),
            V((8, OWN, D), bf16),
            S((2,)),
            S((8,)), S((8,)),
            S((NB, 2)), S((NB, 2)),
            S((NB, 2)), S((NB, 2)),
            S((NB,)), S((NB,)),
            S((NB,)), S((NB,)),
            S((NB, 2)), S((NB, 2)),
            S((NB, 2)), S((NB, 2)),
            S((8,)), S((8,)),
            S((8,)), S((8, NG)), S((8, SPLIT)),
            S((2,)), S((2, NS)),
            S((2,)), S((2, NS)),
            S((8,)), S((8,)),
            S((1,)),
        ],
        compiler_params=pltpu.CompilerParams(
            collective_id=0, has_side_effects=True, vmem_limit_bytes=58 << 20
        ),
        cost_estimate=pl.CostEstimate(flops=4_000_000_000, bytes_accessed=12_000_000, transcendentals=0),
    )(hidden[0], weight[0], target[0], router_prob[0], routes[0].transpose(0, 2, 1), assign.reshape(1, -1))
    return result[None]


def solution(mesh):
    placed = (
        P("client", None, None, "mp"),
        P("client", "mp", None),
        P("client", None, "mp", None),
        P("client", None, "mp"),
        P("client", None, "mp", None),
        P(),
    )
    return jax.shard_map(
        body, mesh=mesh, in_specs=placed, out_specs=P("client", "mp", None), check_vma=False
    )
```
